256 devices in a mesh: stn: 32 (over z, x_lo, core), tm: 8 (over x_hi, y).
Axes of the slice: x: 4 (x_hi: 2, x_lo: 2; x = x_hi * 2 + x_lo), y: 4, z: 8, core: 2. Of those that a mesh axis runs over, the one named last changes fastest.
Arguments:
- voltage: bfloat16 [256, 256, 2, 4096], P('stn', 'tm'), may hold values from -6 to 6
- fir_taps: float32 [16, 4096], replicated, may hold values from -1.5 to 1.5
Outputs:
- visibilities: float32 [2, 256, 32, 2048], P(None, 'stn', None, 'tm')
The draws below stay inside these ranges and needn't reach their ends.
All inputs are finite; a program needn't handle non-finite values.
Results may differ from the reference program's by a relative error of at most 0.0014.
Values may be sent and summed in bfloat16 or wider, within the bound.
A program may use at most 192 MiB of HBM per device.

```python
import math
import jax
import jax.numpy as jnp
from jax import lax

SIG_DEV = 8
SIGNALS = 256
NCH = 4096
CHANS = 2048
TAPS = 16
VISITS = 4
FRAMES = 256
N_STN = 32


def block_levels(own_key, dims, cuts, low, high):
    def one(position, parts):
        draws = jax.random.uniform(jax.random.fold_in(jax.random.fold_in(own_key, 6), position), (parts,), jnp.float32, low / len(cuts), high / len(cuts))
        return jnp.repeat(jnp.exp(draws), dims[position] // parts).reshape((-1,) + (1,) * (len(dims) - position - 1))

    loudness = one(*cuts[0])
    for cut in cuts[1:]:
        loudness = loudness * one(*cut)
    return loudness


def gaussian(rng, dims, deviation, reach, cuts=(), kind=jnp.bfloat16):
    drawn = deviation * jax.random.normal(rng, dims, jnp.float32)
    if cuts:
        drawn = drawn * block_levels(rng, dims, cuts, -0.22, 0.18)
    return jnp.clip(drawn, -reach, reach).astype(kind)


def setup_inputs(seed: int = 0) -> dict:
    keys = jax.random.split(jax.random.key(seed), 3)
    return {
        "voltage": gaussian(keys[0], (SIGNALS, FRAMES, 2, NCH), 1.0, 6.0, ((0, 32), (1, 8))),
        "fir_taps": gaussian(keys[1], (TAPS, NCH), 0.25, 1.5, (), jnp.float32),
    }


def channel_block(block, fir_taps):
    frames_all = block.shape[1]
    extended = jnp.pad(block.astype(jnp.float32), ((0, 0), (TAPS - 1, 0), (0, 0), (0, 0)))
    filtered = fir_taps[0] * extended[:, 0:frames_all]
    for tap_index in range(1, TAPS):
        filtered = filtered + fir_taps[tap_index] * extended[:, tap_index:tap_index + frames_all]
    complex_form = filtered[:, :, 0] + 1j * filtered[:, :, 1]
    spectrum = jnp.fft.fft(complex_form, axis=-1)[..., :CHANS] / math.sqrt(NCH)
    return jnp.stack([jnp.real(spectrum), jnp.imag(spectrum)], axis=2).astype(jnp.bfloat16)

def correlate(own_block, other_block):
    products = jnp.einsum('sfrc,tfqc->rsqtc', own_block.astype(jnp.float32), other_block.astype(jnp.float32))
    real_part = products[0, :, 0] + products[1, :, 1]
    imag_part = products[1, :, 0] - products[0, :, 1]
    return jnp.stack([real_part, imag_part], 0)

def reference(voltage, fir_taps):
    grouped = voltage.reshape(N_STN, SIG_DEV, FRAMES, 2, NCH)
    spectra = lax.map(lambda blk: channel_block(blk, fir_taps), grouped)

    def one_block(block_index):
        own_block = spectra[block_index]
        pieces = []
        for visit_index in range(VISITS):
            partner = ((block_index - visit_index) % N_STN).astype(jnp.int32)
            pieces.append(correlate(own_block, spectra[partner]))
        return jnp.concatenate(pieces, 2) / FRAMES
    blockwise = lax.map(one_block, jnp.arange(N_STN, dtype=jnp.int32))
    return jnp.transpose(blockwise, (1, 0, 2, 3, 4)).reshape(2, SIGNALS, VISITS * SIG_DEV, CHANS)
```

```python
import functools
import math

import jax
import jax.numpy as jnp
import numpy as np
from jax import lax
from jax.experimental import pallas as pl
from jax.experimental.pallas import tpu as pltpu
from jax.sharding import PartitionSpec as P

MESH = pl.DeviceIdType.MESH
TAPS = 16
SIG = 8
FR = 32
EXT = 48
QUAD = 4
TMS = 8
PLANE = QUAD * TMS
NT = (((1,), (1,)), ((), ()))


def split(table):
    high = table.astype(jnp.bfloat16)
    low = (table - high.astype(np.float64)).astype(jnp.bfloat16)
    return high, low


def tables():
    hi = np.arange(32)
    lo = np.arange(128)
    c1 = np.arange(32)
    c2 = np.arange(64)
    angle = 2.0 * math.pi * (np.outer(c1, hi) % 32) / 32.0
    first = np.zeros((2, 32, 32, 2))
    first[0, :, :, 0] = np.cos(angle)
    first[0, :, :, 1] = np.sin(angle)
    first[1, :, :, 0] = -np.sin(angle)
    first[1, :, :, 1] = np.cos(angle)
    high, low = split(first.reshape(64, 64))
    w1 = np.concatenate([high, low, high], axis=1)
    angle = 2.0 * math.pi * np.outer(c1, lo) / 4096.0
    turn = np.stack([np.cos(angle), np.sin(angle)]).astype(np.float32)
    angle = 2.0 * math.pi * (np.outer(c2, lo) % 128) / 128.0
    second = np.zeros((64, 2, 2, 128))
    second[:, 0, 0] = np.cos(angle)
    second[:, 0, 1] = np.sin(angle)
    second[:, 1, 0] = -np.sin(angle)
    second[:, 1, 1] = np.cos(angle)
    high, low = split(second.reshape(128, 256) / 64.0)
    w2 = np.concatenate([high, low], axis=0)
    return w1, turn, w2


def kernel(
    v_hbm, taps_ref, w1_ref, turn_ref, w2_ref, out_ref,
    vbuf, vf, yf, zh, zl, msg, recv, mrg, zrecv, qf, psend, obuf,
    v_sem, send_sem, recv_sem, zsend_sem, zrecv_sem, rsend_sem, rrecv_sem,
):
    stn = lax.axis_index("stn")
    tm = lax.axis_index("tm")
    z = stn // QUAD
    q_me = stn % QUAD
    me = tm * QUAD + q_me
    up = ((z + 1) % 8) * QUAD + q_me
    down = ((z + 7) % 8) * QUAD + q_me

    def place(plane_index):
        return (z * QUAD + plane_index % QUAD, plane_index // QUAD)

    def load(s):
        return pltpu.make_async_copy(v_hbm.at[s], vbuf.at[s], v_sem.at[s])

    for s in range(SIG):
        load(s).start()

    barrier = pltpu.get_barrier_semaphore()

    def greet(j, carry):
        pl.semaphore_signal(barrier, inc=1, device_id=place((me + j) % PLANE), device_id_type=MESH)
        return carry

    lax.fori_loop(1, PLANE, greet, 0)
    pl.semaphore_signal(barrier, inc=1, device_id=(up, tm), device_id_type=MESH)
    pl.semaphore_signal(barrier, inc=1, device_id=(down, tm), device_id_type=MESH)

    def channelise(s):
        load(s).wait()

        def widen(f, carry):
            vf[f] = vbuf[s, f].astype(jnp.float32)
            return carry

        lax.fori_loop(0, FR, widen, 0)

        def fir(g, carry):
            rows = pl.ds(pl.multiple_of(g * 8, 8), 8)
            taps = [taps_ref[m, rows, :] for m in range(TAPS)]
            frames = {}
            for f_out in range(FR + TAPS - 1):
                if f_out < FR:
                    frames[f_out] = vf[f_out, rows, :]
                total = None
                for m in range(TAPS):
                    f_in = f_out - (TAPS - 1) + m
                    if 0 <= f_in < FR:
                        term = taps[m] * frames[f_in]
                        total = term if total is None else total + term
                yf[f_out, rows, :] = total
            return carry

        lax.fori_loop(0, 8, fir, 0)

        def first_stage(pair, carry):
            x = jnp.concatenate([yf[2 * pair], yf[2 * pair + 1]], axis=1)
            high = x.astype(jnp.bfloat16)
            low = (x - high.astype(jnp.float32)).astype(jnp.bfloat16)
            y = jnp.dot(
                w1_ref[...], jnp.concatenate([high, high, low], axis=0),
                preferred_element_type=jnp.float32,
            )
            parts = []
            for j in range(2):
                yr = y[0:32, 128 * j:128 * j + 128]
                yi = y[32:64, 128 * j:128 * j + 128]
                zr = yr * turn_ref[0] + yi * turn_ref[1]
                zi = yi * turn_ref[0] - yr * turn_ref[1]
                parts.append((zr, zi))
            rows = pl.ds(pl.multiple_of(pair * 16, 16), 16)
            for q in range(QUAD):
                for r in range(2):
                    block = jnp.concatenate([parts[0][r][8 * q:8 * q + 8], parts[1][r][8 * q:8 * q + 8]], axis=0)
                    high = block.astype(jnp.bfloat16)
                    zh[q, rows, 128 * r:128 * r + 128] = high
                    zl[q, rows, 128 * r:128 * r + 128] = (block - high.astype(jnp.float32)).astype(jnp.bfloat16)
            return carry

        lax.fori_loop(0, EXT // 2, first_stage, 0)

        for q in range(QUAD):
            full = lax.dot_general(w2_ref[...], zh[q], NT, preferred_element_type=jnp.float32)
            rest = lax.dot_general(w2_ref[0:128, :], zl[q], NT, preferred_element_type=jnp.float32)
            spectra = (full[0:128] + full[128:256] + rest).astype(jnp.bfloat16)
            for t in range(TMS):
                msg[s, t * QUAD + q] = spectra[16 * t:16 * t + 16]

    def send(s):
        def one(j, carry):
            to = (me + j) % PLANE
            pltpu.make_async_remote_copy(
                src_ref=msg.at[s, to], dst_ref=recv.at[s, me],
                send_sem=send_sem.at[s], recv_sem=recv_sem.at[s],
                device_id=place(to), device_id_type=MESH,
            ).start()
            return carry

        pltpu.make_async_copy(msg.at[s, me], recv.at[s, me], recv_sem.at[s]).start()
        lax.fori_loop(1, PLANE, one, 0)

    def pass_up(s):
        return pltpu.make_async_remote_copy(
            src_ref=mrg.at[s, pl.ds(1, 3)], dst_ref=zrecv.at[s],
            send_sem=zsend_sem.at[s], recv_sem=zrecv_sem.at[s],
            device_id=(up, tm), device_id_type=MESH,
        )

    def spread(values, slot, s, tile):
        wide = values.astype(jnp.float32)
        for g in range(2):
            qf[tile, pl.ds(g * 512 + slot * 8 + s, 8, stride=64), :] = wide[8 * g:8 * g + 8]

    def merge(s):
        pltpu.make_async_copy(recv.at[s], recv.at[s], recv_sem.at[s]).wait()
        for q in range(QUAD):
            for t in range(TMS):
                early = recv[s, t * QUAD + q, :, 0:128]
                if t > 0:
                    before = recv[s, (t - 1) * QUAD + q, :, 256:384]
                    early = (early.astype(jnp.float32) + before.astype(jnp.float32)).astype(jnp.bfloat16)
                late = recv[s, t * QUAD + q, :, 128:256]
                mrg[s, q, t, :, 0:128] = early
                mrg[s, q, t, :, 128:256] = late
                spread(early, 3 - q, s, 2 * t)
                spread(late, 3 - q, s, 2 * t + 1)
        pass_up(s).start()

    def merge_passed(s, carry):
        pass_up(s).wait_recv()
        for k in range(3):
            for t in range(TMS):
                for h in range(2):
                    spread(zrecv[s, k, t, :, 128 * h:128 * h + 128], 6 - k, s, 2 * t + h)
        return carry

    yf[EXT - 1] = jnp.zeros((64, 128), jnp.float32)

    def clear(i, carry):
        qf[:, pl.ds(pl.multiple_of(i * 64 + 56, 8), 8), :] = jnp.zeros((16, 8, 128), jnp.float32)
        return carry

    lax.fori_loop(0, 16, clear, 0)

    channelise(0)
    pl.semaphore_wait(barrier, PLANE + 1)
    send(0)

    def step(s, carry):
        @pl.when(s < SIG)
        def _():
            channelise(s)
            send(s)

        @pl.when(s >= 2)
        def _():
            merge(s - 2)

        return carry

    lax.fori_loop(1, SIG + 2, step, 0)
    lax.fori_loop(0, SIG, merge_passed, 0)

    lane = lax.broadcasted_iota(jnp.int32, (1, 2048), 1) % 8
    lane_out = lax.broadcasted_iota(jnp.int32, (1, 128), 1)
    sign = jnp.where(lane_out < 64, 1.0, -1.0).astype(jnp.float32)
    first_half = (lane_out // 32) % 2 == 0

    def gram(c2):
        rows = pl.ds(pl.multiple_of(c2 * 128, 128), 128)
        b = jnp.concatenate([qf[k, rows, :].astype(jnp.bfloat16) for k in range(16)], axis=1)
        a = jnp.concatenate([b[0:32], b[64:96]], axis=0)
        stacked = jnp.concatenate(
            [jnp.where(lane == c1, a, jnp.zeros_like(a)) for c1 in range(8)], axis=0
        )
        out = lax.dot_general(stacked, b, NT, preferred_element_type=jnp.float32)
        return out * (1.0 / 256.0)

    def result(c2lo, i):
        return pltpu.make_async_remote_copy(
            src_ref=psend.at[c2lo, 3 - i], dst_ref=obuf.at[c2lo, q_me],
            send_sem=rsend_sem.at[c2lo], recv_sem=rrecv_sem.at[c2lo],
            device_id=(z * QUAD + i, tm), device_id_type=MESH,
        )

    def correlate(c2lo, carry):
        grams = [gram(c2lo), gram(c2lo + 4)]
        for c1 in range(8):
            packed = []
            for full in grams:
                g0 = full[64 * c1:64 * c1 + 32]
                g1 = full[64 * c1 + 32:64 * c1 + 64]
                packed.append(pltpu.roll(g1, 64, 1) + sign * g0)
            for slot in range(QUAD):
                low = packed[0][8 * slot:8 * slot + 8]
                high = packed[1][8 * slot:8 * slot + 8]
                if slot:
                    low = pltpu.roll(low, 128 - 8 * slot, 1)
                high = pltpu.roll(high, (128 - 8 * slot + 32) % 128, 1)
                psend[c2lo, slot, c1] = jnp.where(first_half, low, high)
        pltpu.make_async_copy(psend.at[c2lo, 3 - q_me], obuf.at[c2lo, q_me], rrecv_sem.at[c2lo]).start()
        for j in range(1, QUAD):
            result(c2lo, (q_me + j) % QUAD).start()
        return carry

    lax.fori_loop(0, 4, correlate, 0)

    for c2lo in range(4):
        pltpu.make_async_copy(obuf.at[c2lo], obuf.at[c2lo], rrecv_sem.at[c2lo]).wait()

    flat = obuf.reshape(4 * QUAD * 8 * SIG, 128)
    for s in range(SIG):
        block = flat[pl.ds(s, 128, stride=8), :].T
        for part in range(2):
            for half in range(2):
                at = (part * 2 + half) * 32
                out_ref[part, s, :, 128 * half:128 * half + 128] = block[at:at + 32]

    def settle(s, carry):
        pltpu.make_async_copy(msg.at[s, pl.ds(0, PLANE - 1)], recv.at[s, pl.ds(0, PLANE - 1)], send_sem.at[s]).wait()
        pass_up(s).wait_send()
        return carry

    lax.fori_loop(0, SIG, settle, 0)
    for c2lo in range(4):
        pltpu.make_async_copy(
            psend.at[c2lo, pl.ds(0, 3)], obuf.at[c2lo, pl.ds(0, 3)], rsend_sem.at[c2lo]
        ).wait()


def local(voltage, fir_taps):
    rows = voltage.reshape(SIG, FR, 2, 32, 128).transpose(0, 1, 3, 2, 4).reshape(SIG, FR, 64, 128)
    taps = jnp.broadcast_to(fir_taps.reshape(TAPS, 32, 1, 128), (TAPS, 32, 2, 128)).reshape(TAPS, 64, 128)
    w1, turn, w2 = tables()
    vmem = pl.BlockSpec(memory_space=pltpu.VMEM)
    return pl.pallas_call(
        kernel,
        out_shape=jax.ShapeDtypeStruct((2, SIG, 32, 256), jnp.float32),
        in_specs=[pl.BlockSpec(memory_space=pl.ANY), vmem, vmem, vmem, vmem],
        out_specs=vmem,
        scratch_shapes=[
            pltpu.VMEM((SIG, FR, 64, 128), jnp.bfloat16),
            pltpu.VMEM((FR, 64, 128), jnp.float32),
            pltpu.VMEM((EXT, 64, 128), jnp.float32),
            pltpu.VMEM((QUAD, EXT * 8, 256), jnp.bfloat16),
            pltpu.VMEM((QUAD, EXT * 8, 256), jnp.bfloat16),
            pltpu.VMEM((SIG, PLANE, 16, 384), jnp.bfloat16),
            pltpu.VMEM((SIG, PLANE, 16, 384), jnp.bfloat16),
            pltpu.VMEM((SIG, QUAD, TMS, 16, 256), jnp.bfloat16),
            pltpu.VMEM((SIG, 3, TMS, 16, 256), jnp.bfloat16),
            pltpu.VMEM((16, 16 * 64, 128), jnp.float32),
            pltpu.VMEM((4, QUAD, 8, SIG, 128), jnp.float32),
            pltpu.VMEM((4, QUAD, 8, SIG, 128), jnp.float32),
            pltpu.SemaphoreType.DMA((SIG,)),
            pltpu.SemaphoreType.DMA((SIG,)),
            pltpu.SemaphoreType.DMA((SIG,)),
            pltpu.SemaphoreType.DMA((SIG,)),
            pltpu.SemaphoreType.DMA((SIG,)),
            pltpu.SemaphoreType.DMA((4,)),
            pltpu.SemaphoreType.DMA((4,)),
        ],
        compiler_params=pltpu.CompilerParams(
            collective_id=0, has_side_effects=True, vmem_limit_bytes=60 * 1024 * 1024
        ),
    )(rows, taps, jnp.asarray(w1), jnp.asarray(turn), jnp.asarray(w2))


def solution(mesh):
    return jax.shard_map(
        local,
        mesh=mesh,
        in_specs=(P("stn", "tm", None, None), P()),
        out_specs=P(None, "stn", None, "tm"),
        check_vma=False,
    )
```

```python
import functools
import math

import jax
import jax.numpy as jnp
import numpy as np
from jax import lax
from jax.experimental import pallas as pl
from jax.experimental.pallas import tpu as pltpu
from jax.sharding import PartitionSpec as P

MESH = pl.DeviceIdType.MESH
TAPS = 16
SIG = 8
FR = 32
EXT = 48
QUAD = 4
TMS = 8
PLANE = QUAD * TMS
GROUP = 16
NT = (((1,), (1,)), ((), ()))


def split(table):
    high = table.astype(jnp.bfloat16)
    low = (table - high.astype(np.float64)).astype(jnp.bfloat16)
    return high, low


def tables():
    hi = np.arange(32)
    lo = np.arange(128)
    c1 = np.arange(32)
    c2 = np.arange(64)
    angle = 2.0 * math.pi * (np.outer(c1, hi) % 32) / 32.0
    first = np.zeros((2, 32, 32, 2))
    first[0, :, :, 0] = np.cos(angle)
    first[0, :, :, 1] = np.sin(angle)
    first[1, :, :, 0] = -np.sin(angle)
    first[1, :, :, 1] = np.cos(angle)
    high, low = split(first.reshape(64, 64))
    w1 = np.concatenate([high, low, high], axis=1)
    angle = 2.0 * math.pi * np.outer(c1, lo) / 4096.0
    turn = np.stack([np.cos(angle), np.sin(angle)]).astype(np.float32)
    angle = 2.0 * math.pi * (np.outer(c2, lo) % 128) / 128.0
    second = np.zeros((64, 2, 2, 128))
    second[:, 0, 0] = np.cos(angle)
    second[:, 0, 1] = np.sin(angle)
    second[:, 1, 0] = -np.sin(angle)
    second[:, 1, 1] = np.cos(angle)
    high, low = split(second.reshape(128, 256) / 64.0)
    w2 = np.concatenate([high, low], axis=0)
    return w1, turn, w2


def kernel(
    v_hbm, fir_ref, w1_ref, turn_ref, w2_ref, out_ref,
    taps_ref, vbuf, vf, yf, zh, zl, msg, recv, mrg, zrecv, qf, psend, obuf,
    v_sem, send_sem, recv_sem, zsend_sem, zrecv_sem, rsend_sem, rrecv_sem,
):
    stn = lax.axis_index("stn")
    tm = lax.axis_index("tm")
    z = stn // QUAD
    q_me = stn % QUAD
    me = tm * QUAD + q_me
    up = ((z + 1) % 8) * QUAD + q_me
    down = ((z + 7) % 8) * QUAD + q_me

    def place(plane_index):
        return (z * QUAD + plane_index % QUAD, plane_index // QUAD)

    def load(s):
        return pltpu.make_async_copy(v_hbm.at[s], vbuf.at[s], v_sem.at[s])

    for s in range(SIG):
        load(s).start()

    barrier = pltpu.get_barrier_semaphore()

    def greet(j, carry):
        pl.semaphore_signal(barrier, inc=1, device_id=place((me + j) % PLANE), device_id_type=MESH)
        return carry

    lax.fori_loop(1, PLANE, greet, 0)
    pl.semaphore_signal(barrier, inc=1, device_id=(up, tm), device_id_type=MESH)
    pl.semaphore_signal(barrier, inc=1, device_id=(down, tm), device_id_type=MESH)

    def channelise(s):
        load(s).wait()

        def widen(f, carry):
            vf[f] = vbuf[s, f].astype(jnp.float32)
            return carry

        lax.fori_loop(0, FR, widen, 0)

        def fir(g, carry):
            rows = pl.ds(pl.multiple_of(g * 8, 8), 8)
            taps = [taps_ref[pl.ds(pl.multiple_of(g * 8 + m * 64, 8), 8), :] for m in range(TAPS)]
            frames = {}
            for f_out in range(FR + TAPS - 1):
                if f_out < FR:
                    frames[f_out] = vf[f_out, rows, :]
                total = None
                for m in range(TAPS):
                    f_in = f_out - (TAPS - 1) + m
                    if 0 <= f_in < FR:
                        term = taps[m] * frames[f_in]
                        total = term if total is None else total + term
                yf[f_out, rows, :] = total
            return carry

        lax.fori_loop(0, 8, fir, 0)

        def first_stage(step, carry):
            x = jnp.concatenate([yf[step * GROUP + j] for j in range(GROUP)], axis=1)
            high = x.astype(jnp.bfloat16)
            low = (x - high.astype(jnp.float32)).astype(jnp.bfloat16)
            y = jnp.dot(
                w1_ref[...], jnp.concatenate([high, high, low], axis=0),
                preferred_element_type=jnp.float32,
            )
            parts = []
            for j in range(GROUP):
                yr = y[0:32, 128 * j:128 * j + 128]
                yi = y[32:64, 128 * j:128 * j + 128]
                zr = yr * turn_ref[0] + yi * turn_ref[1]
                zi = yi * turn_ref[0] - yr * turn_ref[1]
                parts.append((zr, zi))
            rows = pl.ds(pl.multiple_of(step * (8 * GROUP), 8 * GROUP), 8 * GROUP)
            for q in range(QUAD):
                for r in range(2):
                    block = jnp.concatenate([part[r][8 * q:8 * q + 8] for part in parts], axis=0)
                    high = block.astype(jnp.bfloat16)
                    zh[q, rows, 128 * r:128 * r + 128] = high
                    zl[q, rows, 128 * r:128 * r + 128] = (block - high.astype(jnp.float32)).astype(jnp.bfloat16)
            return carry

        lax.fori_loop(0, EXT // GROUP, first_stage, 0)

        for q in range(QUAD):
            full = lax.dot_general(w2_ref[...], zh[q], NT, preferred_element_type=jnp.float32)
            rest = lax.dot_general(w2_ref[0:128, :], zl[q], NT, preferred_element_type=jnp.float32)
            spectra = (full[0:128] + full[128:256] + rest).astype(jnp.bfloat16)
            for t in range(TMS):
                msg[s, t * QUAD + q] = spectra[16 * t:16 * t + 16]

    def send(s):
        def one(j, carry):
            to = (me + j) % PLANE
            pltpu.make_async_remote_copy(
                src_ref=msg.at[s, to], dst_ref=recv.at[s, me],
                send_sem=send_sem.at[s], recv_sem=recv_sem.at[s],
                device_id=place(to), device_id_type=MESH,
            ).start()
            return carry

        pltpu.make_async_copy(msg.at[s, me], recv.at[s, me], recv_sem.at[s]).start()
        lax.fori_loop(1, PLANE, one, 0)

    def pass_up(s):
        return pltpu.make_async_remote_copy(
            src_ref=mrg.at[s], dst_ref=zrecv.at[s],
            send_sem=zsend_sem.at[s], recv_sem=zrecv_sem.at[s],
            device_id=(up, tm), device_id_type=MESH,
        )

    def spread(wide, slot, s, tile):
        for g in range(2):
            qf[tile, pl.ds(g * 512 + slot * 8 + s, 8, stride=64), :] = wide[8 * g:8 * g + 8]

    lane_of = lax.broadcasted_iota(jnp.int32, (1, 128), 1)

    def exchange(tiles, bit, distance):
        clear = (lane_of // distance) % 2 == 0
        out = list(tiles)
        for k in range(8):
            if (k // bit) % 2 == 0:
                a, b = tiles[k], tiles[k + bit]
                out[k] = jnp.where(clear, a, pltpu.roll(b, distance, 1))
                out[k + bit] = jnp.where(clear, pltpu.roll(a, 128 - distance, 1), b)
        return out

    def merge(s):
        pltpu.make_async_copy(recv.at[s], recv.at[s], recv_sem.at[s]).wait()
        for q in range(QUAD):
            for side in range(2):
                tiles = []
                for t in range(4 * side, 4 * side + 4):
                    early = recv[s, t * QUAD + q, :, 0:128].astype(jnp.float32)
                    if t > 0:
                        before = recv[s, (t - 1) * QUAD + q, :, 256:384].astype(jnp.float32)
                        early = (early + before).astype(jnp.bfloat16).astype(jnp.float32)
                    tiles += [early, recv[s, t * QUAD + q, :, 128:256].astype(jnp.float32)]
                tiles = exchange(tiles, 1, 4)
                tiles = exchange(tiles, 2, 2)
                tiles = exchange(tiles, 4, 1)
                for k in range(8):
                    c1 = (k % 2) * 4 + (k // 2 % 2) * 2 + k // 4
                    spread(tiles[k], 3 - q, s, 2 * c1 + side)
                    if q > 0:
                        mrg[s, q - 1, 2 * c1 + side] = tiles[k].astype(jnp.bfloat16)
        pass_up(s).start()

    def merge_passed(s, carry):
        pass_up(s).wait_recv()
        for k in range(3):
            for tile in range(16):
                spread(zrecv[s, k, tile].astype(jnp.float32), 6 - k, s, tile)
        return carry

    for hi in range(32):
        for g in range(2):
            taps = fir_ref[8 * g:8 * g + 8, 128 * hi:128 * hi + 128]
            for r in range(2):
                taps_ref[pl.ds(512 * g + 2 * hi + r, 8, stride=64), :] = taps

    yf[EXT - 1] = jnp.zeros((64, 128), jnp.float32)

    def clear(i, carry):
        qf[:, pl.ds(pl.multiple_of(i * 64 + 56, 8), 8), :] = jnp.zeros((16, 8, 128), jnp.float32)
        return carry

    lax.fori_loop(0, 16, clear, 0)

    channelise(0)
    pl.semaphore_wait(barrier, PLANE + 1)
    send(0)

    def step(s, carry):
        @pl.when(s < SIG)
        def _():
            channelise(s)
            send(s)

        @pl.when(s >= 2)
        def _():
            merge(s - 2)

        return carry

    lax.fori_loop(1, SIG + 2, step, 0)
    lax.fori_loop(0, SIG, merge_passed, 0)

    sign = jnp.where(lane_of < 64, 1.0, -1.0).astype(jnp.float32)
    first_half = (lane_of // 32) % 2 == 0

    def gram(c2, c1):
        rows = pl.ds(pl.multiple_of(c2 * 128, 128), 128)
        b = jnp.concatenate([qf[2 * c1 + side, rows, :].astype(jnp.bfloat16) for side in range(2)], axis=1)
        a = jnp.concatenate([b[0:32], b[64:96]], axis=0)
        out = lax.dot_general(a, b, NT, preferred_element_type=jnp.float32) * (1.0 / 256.0)
        return pltpu.roll(out[32:64], 64, 1) + sign * out[0:32]

    def result(c2lo, i):
        return pltpu.make_async_remote_copy(
            src_ref=psend.at[c2lo, 3 - i], dst_ref=obuf.at[c2lo, q_me],
            send_sem=rsend_sem.at[c2lo], recv_sem=rrecv_sem.at[c2lo],
            device_id=(z * QUAD + i, tm), device_id_type=MESH,
        )

    def correlate(c2lo, carry):
        for c1 in range(8):
            packed = [gram(c2lo, c1), gram(c2lo + 4, c1)]
            for slot in range(QUAD):
                low = packed[0][8 * slot:8 * slot + 8]
                high = packed[1][8 * slot:8 * slot + 8]
                if slot:
                    low = pltpu.roll(low, 128 - 8 * slot, 1)
                high = pltpu.roll(high, (128 - 8 * slot + 32) % 128, 1)
                psend[c2lo, slot, c1] = jnp.where(first_half, low, high)
        pltpu.make_async_copy(psend.at[c2lo, 3 - q_me], obuf.at[c2lo, q_me], rrecv_sem.at[c2lo]).start()
        for j in range(1, QUAD):
            result(c2lo, (q_me + j) % QUAD).start()
        return carry

    lax.fori_loop(0, 4, correlate, 0)

    for c2lo in range(4):
        pltpu.make_async_copy(obuf.at[c2lo], obuf.at[c2lo], rrecv_sem.at[c2lo]).wait()

    flat = obuf.reshape(4 * QUAD * 8 * SIG, 128)
    for s in range(SIG):
        block = flat[pl.ds(s, 128, stride=8), :].T
        for part in range(2):
            for half in range(2):
                at = (part * 2 + half) * 32
                out_ref[part, s, :, 128 * half:128 * half + 128] = block[at:at + 32]

    def settle(s, carry):
        pltpu.make_async_copy(msg.at[s, pl.ds(0, PLANE - 1)], recv.at[s, pl.ds(0, PLANE - 1)], send_sem.at[s]).wait()
        pass_up(s).wait_send()
        return carry

    lax.fori_loop(0, SIG, settle, 0)
    for c2lo in range(4):
        pltpu.make_async_copy(
            psend.at[c2lo, pl.ds(0, 3)], obuf.at[c2lo, pl.ds(0, 3)], rsend_sem.at[c2lo]
        ).wait()


def local(voltage, fir_taps):
    rows = voltage.reshape(SIG, FR, 2, 32, 128).transpose(0, 1, 3, 2, 4).reshape(SIG, FR, 64, 128)
    w1, turn, w2 = tables()
    vmem = pl.BlockSpec(memory_space=pltpu.VMEM)
    return pl.pallas_call(
        kernel,
        out_shape=jax.ShapeDtypeStruct((2, SIG, 32, 256), jnp.float32),
        in_specs=[pl.BlockSpec(memory_space=pl.ANY), vmem, vmem, vmem, vmem],
        out_specs=vmem,
        scratch_shapes=[
            pltpu.VMEM((TAPS * 64, 128), jnp.float32),
            pltpu.VMEM((SIG, FR, 64, 128), jnp.bfloat16),
            pltpu.VMEM((FR, 64, 128), jnp.float32),
            pltpu.VMEM((EXT, 64, 128), jnp.float32),
            pltpu.VMEM((QUAD, EXT * 8, 256), jnp.bfloat16),
            pltpu.VMEM((QUAD, EXT * 8, 256), jnp.bfloat16),
            pltpu.VMEM((SIG, PLANE, 16, 384), jnp.bfloat16),
            pltpu.VMEM((SIG, PLANE, 16, 384), jnp.bfloat16),
            pltpu.VMEM((SIG, 3, 16, 16, 128), jnp.bfloat16),
            pltpu.VMEM((SIG, 3, 16, 16, 128), jnp.bfloat16),
            pltpu.VMEM((16, 16 * 64, 128), jnp.float32),
            pltpu.VMEM((4, QUAD, 8, SIG, 128), jnp.float32),
            pltpu.VMEM((4, QUAD, 8, SIG, 128), jnp.float32),
            pltpu.SemaphoreType.DMA((SIG,)),
            pltpu.SemaphoreType.DMA((SIG,)),
            pltpu.SemaphoreType.DMA((SIG,)),
            pltpu.SemaphoreType.DMA((SIG,)),
            pltpu.SemaphoreType.DMA((SIG,)),
            pltpu.SemaphoreType.DMA((4,)),
            pltpu.SemaphoreType.DMA((4,)),
        ],
        compiler_params=pltpu.CompilerParams(
            collective_id=0, has_side_effects=True, vmem_limit_bytes=60 * 1024 * 1024
        ),
    )(rows, fir_taps, jnp.asarray(w1), jnp.asarray(turn), jnp.asarray(w2))


def solution(mesh):
    return jax.shard_map(
        local,
        mesh=mesh,
        in_specs=(P("stn", "tm", None, None), P()),
        out_specs=P(None, "stn", None, "tm"),
        check_vma=False,
    )
```
